32 devices in a mesh: dp: 2 (over core), order: 8 (over z, y), ens: 2 (over x).
Axes of the slice: x: 2, y: 2, z: 4, core: 2. Of those that a mesh axis runs over, the one named last changes fastest.
Arguments:
- fourier: bfloat16 [2, 16, 320, 40960], P('dp', 'ens', 'order'), may hold values from -20 to 20
- analysis: bfloat16 [320, 320, 320], P(None, 'order'), may hold values from -0.3125 to 0.3125
- target: bfloat16 [2, 320, 40960], P('dp', 'ens', 'order'), may hold values from -6 to 6
- band_ids: int32 [320, 320], P('ens', 'order'), may hold values from 0 to 15, as said below
- partners: int32 [16, 4], replicated, may hold values from 0 to 15, as said below
- band_cotangent: float32 [2, 16], replicated, may hold values from 0.5 to 4
Outputs:
- grad_fourier: bfloat16 [2, 16, 320, 40960], P('dp', 'ens', 'order')
- grad_analysis: float32 [320, 320, 320], P(('dp', 'ens'), 'order')
- loss_bands: float32 [16], replicated
The draws below stay inside these ranges and needn't reach their ends.
Inputs may be any that keep to these rules, and one draw needn't show every extreme that they name: band_ids[l,m] depends on l only, never falls as l grows, starts at 0 and takes every band from 0 to 15. `partners`: each row names 4 different members, none equal to the row's own member.
All inputs are finite; a program needn't handle non-finite values.
Results may differ from the reference program's by a relative error of at most 0.0085.
Values may be sent and summed in bfloat16 or wider, within the bound.
A program may use at most 256 MiB of HBM per device.

```python
import math
import jax
import jax.numpy as jnp
from jax import lax

MEMBERS = 16
NLAT = 320
L = 320
C = 64
NBANDS = 16
PARTNERS = 4
MM = 320
B = 2


def blocked_factor(key, count, low):
    block = max(count // 16, 1)
    groups = (count + block - 1) // block
    first, second = jax.random.split(key, 2)
    coarse = jnp.exp(jax.random.uniform(first, (groups,), jnp.float32, math.log(low), 0.0))
    rough = jax.random.uniform(second, (count,), jnp.float32, 0.7, 1.4)
    return jnp.repeat(coarse, block)[:count] * rough


def draw_fourier(key, part):
    first, second, third, fourth, fifth, sixth = jax.random.split(key, 6)
    shape = (B, MEMBERS, NLAT, MM * 2 * C)
    channel_scale = jnp.exp(jax.random.uniform(second, (C,), jnp.float32, 0.0, math.log(10.0)))
    row_scale = jnp.exp(jax.random.uniform(third, (NLAT,), jnp.float32, 0.0, math.log(10.0)))
    scale = row_scale[:, None, None] * channel_scale[None, None, :] / 3.0
    scale = jnp.broadcast_to(scale, (NLAT, MM * 2, C)).reshape(NLAT, MM * 2 * C)
    order_spread = blocked_factor(fifth, MM, 0.1)
    row_spread = blocked_factor(sixth, NLAT, 0.3)
    spread = row_spread[:, None, None] * order_spread[None, :, None]
    spread = jnp.broadcast_to(spread, (NLAT, MM, 2 * C)).reshape(NLAT, MM * 2 * C)
    common = jax.random.normal(fourth, (B, 1, NLAT, MM * 2 * C), jnp.float32)
    individual = jax.random.normal(first, shape, jnp.float32)
    base = 0.5 * common + spread[None, None] * individual
    values = jnp.clip(base, -6.0, 6.0) * scale[None, None]
    return jnp.clip(values, -20.0, 20.0).astype(jnp.bfloat16)


def draw_band_ids(key, part):
    shuffled = jax.random.permutation(key, L - 1)[:NBANDS - 1] + 1
    cuts = jnp.sort(shuffled)
    degrees = jnp.arange(L, dtype=jnp.int32)
    band = jnp.sum((degrees[:, None] >= cuts[None, :]).astype(jnp.int32), axis=1)
    return jnp.broadcast_to(band[:, None], (L, MM)).astype(jnp.int32)


def draw_partners(key, part):
    scores = jax.random.randint(key, (MEMBERS, MEMBERS - 1), 0, 1 << 20) * MEMBERS + jnp.arange(MEMBERS - 1, dtype=jnp.int32)[None, :]
    picks = jnp.argsort(scores, axis=1)[:, :PARTNERS] + 1
    return ((jnp.arange(MEMBERS, dtype=jnp.int32)[:, None] + picks) % MEMBERS).astype(jnp.int32)


def steps_of(own_key, dims, shards, least, high):
    def one(dim, parts):
        heights = jax.random.uniform(jax.random.fold_in(jax.random.fold_in(own_key, 6), dim), (parts,), jnp.float32, least / len(shards), high / len(shards))
        return jnp.repeat(jnp.exp(heights), dims[dim] // parts).reshape((-1,) + (1,) * (len(dims) - dim - 1))

    gain = one(*shards[0])
    for cut in shards[1:]:
        gain = gain * one(*cut)
    return gain


def centred(key, dims, deviation, limit, cuts=(), held_as=jnp.bfloat16):
    entries = deviation * jax.random.normal(key, dims, jnp.float32)
    if cuts:
        entries = entries * steps_of(key, dims, cuts, -0.22, 0.18)
    return jnp.clip(entries, -limit, limit).astype(held_as)


def setup_inputs(seed: int = 0) -> dict:
    splits = jax.random.split(jax.random.key(seed), 7)
    fourier = draw_fourier(jax.random.fold_in(splits[6], 71), 0)
    analysis = centred(splits[1], (NLAT, MM, L), NLAT ** -0.5, 0.3125, ((1, 8),))
    target = centred(splits[2], (B, L, MM * 2 * C), 1.0, 6.0, ((0, 2), (1, 2), (2, 8)))
    band_ids = draw_band_ids(jax.random.fold_in(splits[6], 71), 0)
    partners = draw_partners(jax.random.fold_in(splits[6], 71), 0)
    band_cotangent = jnp.clip(jnp.exp(jax.random.uniform(splits[5], (B, NBANDS), jnp.float32, math.log(0.5), math.log(4.0))), 0.5, 4.0)
    return {"fourier": fourier, "analysis": analysis, "target": target, "band_ids": band_ids, "partners": partners, "band_cotangent": band_cotangent}


HIGHEST = lax.Precision.HIGHEST
EPSILON = 1e-06
WEIGHT_RATIO = 1.0 / 64.0

def band_terms(grams, partners, cotangent):
    diagonal_part = jnp.diagonal(grams, axis1=2, axis2=3)
    squared = diagonal_part[..., :, None] + diagonal_part[..., None, :] - 2.0 * grams
    distance = jnp.sqrt(squared + EPSILON)
    member_ids = jnp.arange(MEMBERS, dtype=jnp.int32)
    counts = lax.optimization_barrier(jnp.sum((partners[:, :, None] == member_ids[None, None, :]).astype(jnp.float32), axis=1))
    obs_dist = distance[:, :, :MEMBERS, MEMBERS]
    pair_dist = distance[:, :, :MEMBERS, :MEMBERS]
    scores = lax.optimization_barrier(jnp.mean(obs_dist, axis=-1)) - lax.optimization_barrier(jnp.sum(counts * pair_dist, axis=(-2, -1))) / (2.0 * MEMBERS * PARTNERS)
    scaled = cotangent * (16.0 * MEMBERS * NLAT)
    symmetric = counts + counts.T
    obs_weight = scaled[..., None] / (MEMBERS * obs_dist)
    pair_weight = scaled[..., None, None] * symmetric / (2.0 * MEMBERS * PARTNERS * pair_dist)
    identity = jnp.eye(MEMBERS, dtype=jnp.float32)
    member_part = pair_weight + identity * (obs_weight - lax.optimization_barrier(jnp.sum(pair_weight, axis=-1)))[..., None]
    mixing = jnp.concatenate([member_part, -obs_weight[..., None]], axis=-1)
    return (scores, mixing)

def reference(fourier, analysis, target, band_ids, partners, band_cotangent):
    width = 2 * C
    grid = fourier.reshape(B, MEMBERS, NLAT, MM, width)
    observed_all = target.reshape(B, L, MM, width)
    degrees = jnp.arange(L, dtype=jnp.int32)
    band_range = jnp.arange(NBANDS, dtype=jnp.int32)
    order_range = jnp.arange(MM, dtype=jnp.int32)

    def stacked_at(order):
        grid_m = lax.dynamic_index_in_dim(grid, order, 3, keepdims=False)
        weight_m = lax.dynamic_index_in_dim(analysis, order, 1, keepdims=False)
        spec = jnp.einsum('bitq,tl->bilq', grid_m.astype(jnp.float32), weight_m.astype(jnp.float32), precision=HIGHEST)
        keep = degrees >= order
        spec = jnp.where(keep[None, None, :, None], spec, 0.0).astype(jnp.bfloat16)
        observed = lax.dynamic_index_in_dim(observed_all, order, 2, keepdims=False)
        observed = jnp.where(keep[None, :, None], observed, jnp.zeros((), jnp.bfloat16))
        stacked = jnp.concatenate([spec, observed[:, None]], axis=1)
        column = lax.dynamic_index_in_dim(band_ids, order, 1, keepdims=False)
        one_hot = (column[:, None] == band_range[None, :]).astype(jnp.float32)
        return (grid_m, weight_m, stacked, one_hot)

    def gram_step(total, order):
        grid_m, weight_m, stacked, one_hot = stacked_at(order)
        values = stacked.astype(jnp.float32)
        terms = jnp.einsum('bilq,bjlq->bijl', values, values, precision=HIGHEST)
        return (total + jnp.einsum('bijl,lk->bkij', terms, one_hot, precision=HIGHEST), None)
    start = jnp.zeros((B, NBANDS, MEMBERS + 1, MEMBERS + 1), jnp.float32)
    grams, unused = lax.scan(gram_step, start, order_range)
    scores, mixing = band_terms(grams, partners, band_cotangent)
    loss_bands = lax.optimization_barrier(jnp.sum(band_cotangent * scores, axis=0))

    def grad_step(order):
        grid_m, weight_m, stacked, one_hot = stacked_at(order)
        spread = jnp.einsum('lk,bkij->blij', one_hot, mixing, precision=HIGHEST)
        grad_spec = jnp.einsum('blij,bjlq->bilq', spread, stacked.astype(jnp.float32), precision=HIGHEST).astype(jnp.bfloat16)
        grad_values = grad_spec.astype(jnp.float32)
        grid_grad = jnp.einsum('bilq,tl->bitq', grad_values, weight_m.astype(jnp.float32), precision=HIGHEST).astype(jnp.bfloat16)
        weight_grad = jnp.einsum('bitq,bilq->tl', grid_m.astype(jnp.float32), grad_values, precision=HIGHEST) * WEIGHT_RATIO
        return (grid_grad, weight_grad)
    grid_grads, weight_grads = lax.map(grad_step, order_range)
    grad_fourier = jnp.transpose(grid_grads, (1, 2, 3, 0, 4)).reshape(B, MEMBERS, NLAT, MM * width)
    grad_analysis = jnp.transpose(weight_grads, (1, 0, 2))
    return (grad_fourier, grad_analysis, loss_bands)
```

```python
import functools

import jax
import jax.numpy as jnp
from jax import lax
from jax.experimental import pallas as pl
from jax.experimental.pallas import tpu as pltpu
from jax.sharding import PartitionSpec as P

MEMBERS = 16
NLAT = 320
L = 320
C = 64
NBANDS = 16
PARTNERS = 4


HIGHEST = lax.Precision.HIGHEST
EPSILON = 1e-06
WEIGHT_RATIO = 1.0 / 64.0


def band_terms(grams, partners, cotangent):
    diagonal_part = jnp.diagonal(grams, axis1=2, axis2=3)
    squared = diagonal_part[..., :, None] + diagonal_part[..., None, :] - 2.0 * grams
    distance = jnp.sqrt(squared + EPSILON)
    member_ids = jnp.arange(MEMBERS, dtype=jnp.int32)
    counts = jnp.sum(
        (partners[:, :, None] == member_ids[None, None, :]).astype(jnp.float32), axis=1
    )
    obs_dist = distance[:, :, :MEMBERS, MEMBERS]
    pair_dist = distance[:, :, :MEMBERS, :MEMBERS]
    scores = jnp.mean(obs_dist, axis=-1) - jnp.sum(counts * pair_dist, axis=(-2, -1)) / (
        2.0 * MEMBERS * PARTNERS
    )
    scaled = cotangent * (16.0 * MEMBERS * NLAT)
    symmetric = counts + counts.T
    obs_weight = scaled[..., None] / (MEMBERS * obs_dist)
    pair_weight = scaled[..., None, None] * symmetric / (2.0 * MEMBERS * PARTNERS * pair_dist)
    identity = jnp.eye(MEMBERS, dtype=jnp.float32)
    member_part = pair_weight + identity * (obs_weight - jnp.sum(pair_weight, axis=-1))[..., None]
    mixing = jnp.concatenate([member_part, -obs_weight[..., None]], axis=-1)
    return (scores, mixing)


def body(fourier, analysis, target, band_ids, partners, band_cotangent):
    samples = fourier.shape[0]
    own_members = fourier.shape[1]
    orders = analysis.shape[1]
    width = 2 * C
    degrees_here = band_ids.shape[0]
    order_start = lax.axis_index("order") * orders
    degree_start = lax.axis_index("ens") * degrees_here
    order_index = order_start + jnp.arange(orders, dtype=jnp.int32)
    all_degrees = jnp.arange(L, dtype=jnp.int32)
    keep_all = all_degrees[:, None] >= order_index[None, :]
    local_degrees = degree_start + jnp.arange(degrees_here, dtype=jnp.int32)
    keep_here = local_degrees[:, None] >= order_index[None, :]
    rows = lax.all_to_all(fourier, "order", split_axis=3, concat_axis=2, tiled=True)
    items = rows.shape[1]
    grid = rows.reshape(samples, items, NLAT, orders, width)
    spec = jnp.einsum("bitmq,tml->bilmq", grid, analysis, preferred_element_type=jnp.float32)
    spec = jnp.where(keep_all[None, None, :, :, None], spec, 0.0).astype(jnp.bfloat16)
    grid_rows = rows
    spectra = spec.reshape(samples, items, L, orders * width)
    gathered = lax.all_to_all(spectra, "ens", split_axis=2, concat_axis=1, tiled=True)
    predicted = gathered.reshape(samples, MEMBERS, degrees_here, orders, width)
    observed = target.reshape(samples, degrees_here, orders, width)
    observed = jnp.where(keep_here[None, :, :, None], observed, jnp.zeros((), jnp.bfloat16))
    stacked = jnp.concatenate([predicted, observed[:, None]], axis=1)
    pair_terms = jnp.einsum(
        "bilmq,bjlmq->bijlm", stacked, stacked, preferred_element_type=jnp.float32
    )
    band_range = jnp.arange(NBANDS, dtype=jnp.int32)
    one_hot = (band_ids[:, :, None] == band_range[None, None, :]).astype(jnp.float32)
    grams = jnp.einsum("bijlm,lmk->bkij", pair_terms, one_hot, precision=HIGHEST)
    sample_start = lax.axis_index("dp") * samples
    grams = lax.psum(grams, ("order", "ens"))
    cotangent = lax.dynamic_slice_in_dim(band_cotangent, sample_start, samples, 0)
    scores, mixing = band_terms(grams, partners, cotangent)
    loss_bands = lax.psum(jnp.sum(cotangent * scores, axis=0), "dp")
    spread = jnp.einsum("lmk,bkij->blmij", one_hot, mixing, precision=HIGHEST)
    grad_spec = jnp.einsum(
        "blmij,bjlmq->bilmq", spread, stacked.astype(jnp.float32), precision=HIGHEST
    ).astype(jnp.bfloat16)
    grad_spec = grad_spec.reshape(samples, MEMBERS, degrees_here, orders * width)
    returned = lax.all_to_all(grad_spec, "ens", split_axis=1, concat_axis=2, tiled=True)
    back = returned.reshape(samples, own_members, L, orders, width)
    grid_own = grid_rows.reshape(samples, own_members, NLAT, orders, width)
    rows = grid_own
    halves = lax.psum_scatter(
        (
            jnp.einsum("bitmq,bilmq->tml", rows, back, preferred_element_type=jnp.float32)
            * WEIGHT_RATIO
        ).astype(jnp.bfloat16),
        "dp",
        scatter_dimension=0,
        tiled=True,
    )
    grad_analysis = lax.psum_scatter(halves, "ens", scatter_dimension=0, tiled=True).astype(
        jnp.float32
    )
    grid_grad = jnp.einsum(
        "bilmq,tml->bitmq", back, analysis, preferred_element_type=jnp.float32
    ).astype(jnp.bfloat16)
    grid_grad = grid_grad.reshape(samples, own_members, NLAT, orders * width)
    grad_fourier = lax.all_to_all(grid_grad, "order", split_axis=2, concat_axis=3, tiled=True)
    return (grad_fourier, grad_analysis, loss_bands)


MESH = pl.DeviceIdType.MESH
LANES = 128
BLOCK = 16
ROWS = MEMBERS * BLOCK
PAIR = 2
VMEM_LIMIT = 64000 * 1024


def my_place():
    return lax.axis_index("dp"), lax.axis_index("order"), lax.axis_index("ens")


def other_places(orders, enses):
    core, order, ens = my_place()
    places = []
    for step in range(1, orders * enses):
        flat = lax.rem(order * enses + ens + step, orders * enses)
        places.append((core, flat // enses, lax.rem(flat, enses)))
    return places


def greet(places):
    barrier = pltpu.get_barrier_semaphore()
    for place in places:
        pl.semaphore_signal(barrier, inc=1, device_id=place, device_id_type=MESH)
    pl.semaphore_wait(barrier, len(places))


def gather_kernel(
    orders, enses, fourier, target, onehot, grid, observed, bands, held, held_obs, held_hot,
    send, recv, send_obs, recv_obs, own_sem
):
    core, order, ens = my_place()
    members, rows = fourier.shape[0], fourier.shape[1]
    width = grid.shape[2]
    degrees = target.shape[0]
    places = other_places(orders, enses)
    greet(places)
    copies = []

    def columns(flat):
        return pl.ds(pl.multiple_of(flat * width, LANES), width)

    grid_to = grid.at[pl.ds(ens * members, members), pl.ds(order * rows, rows)]
    obs_to = observed.at[pl.ds(ens * degrees, degrees)]
    hot_to = bands.at[pl.ds(ens * degrees, degrees)]
    for step in range(1, enses):
        other = lax.rem(ens + step, enses)
        place = (core, order, other)
        for k, (source, goal) in enumerate(
            ((target.at[:, columns(other)], obs_to), (onehot, hot_to))
        ):
            copies.append(
                pltpu.make_async_remote_copy(
                    source, goal, send_obs.at[step, k], recv_obs.at[step, k],
                    device_id=place, device_id_type=MESH,
                )
            )
            copies[-1].start()
    for step, place in enumerate(places):
        copies.append(
            pltpu.make_async_remote_copy(
                fourier.at[:, :, columns(place[1] * enses + place[2])], grid_to,
                send.at[step], recv.at[step], device_id=place, device_id_type=MESH,
            )
        )
        copies[-1].start()
    own = (
        (fourier.at[:, :, columns(order * enses + ens)], held, grid_to),
        (target.at[:, columns(ens)], held_obs, obs_to),
        (onehot, held_hot, hot_to),
    )
    first = [pltpu.make_async_copy(a, b, own_sem.at[0, k]) for k, (a, b, _) in enumerate(own)]
    second = [pltpu.make_async_copy(b, c, own_sem.at[1, k]) for k, (_, b, c) in enumerate(own)]
    for copy in first:
        copy.start()
    for one, two in zip(first, second):
        one.wait()
        two.start()
    for copy in second:
        copy.wait()
    for copy in copies:
        copy.wait()


def gather_rows(orders, enses, fourier, target, onehot):
    members, rows, columns = fourier.shape
    width = columns // (orders * enses)
    degrees = target.shape[0]
    peers = orders * enses - 1
    anywhere = pl.BlockSpec(memory_space=pl.ANY)
    return pl.pallas_call(
        functools.partial(gather_kernel, orders, enses),
        out_shape=(
            jax.ShapeDtypeStruct((members * enses, rows * orders, width), fourier.dtype),
            jax.ShapeDtypeStruct((degrees * enses, width), target.dtype),
            jax.ShapeDtypeStruct((degrees * enses, LANES), onehot.dtype),
        ),
        in_specs=[anywhere] * 3,
        out_specs=(anywhere,) * 3,
        scratch_shapes=[
            pltpu.VMEM((members, rows, width), fourier.dtype),
            pltpu.VMEM((degrees, width), target.dtype),
            pltpu.VMEM((degrees, LANES), onehot.dtype),
            pltpu.SemaphoreType.DMA((peers,)),
            pltpu.SemaphoreType.DMA((peers,)),
            pltpu.SemaphoreType.DMA((enses, 2)),
            pltpu.SemaphoreType.DMA((enses, 2)),
            pltpu.SemaphoreType.DMA((2, 3)),
        ],
        compiler_params=pltpu.CompilerParams(
            collective_id=0, has_side_effects=True, vmem_limit_bytes=VMEM_LIMIT
        ),
        name="gather_rows",
    )(fourier, target, onehot)


def scatter_kernel(
    orders, enses, gradient, weight_grad, home, shares, held, held_share,
    send, recv, send_share, recv_share, own_sem
):
    core, order, ens = my_place()
    members, rows = home.shape[0], home.shape[1]
    width = gradient.shape[2]
    part = shares.shape[2]
    places = other_places(orders, enses)
    partners = [(1 - core, order, lax.rem(ens + step, enses)) for step in range(enses)]
    greet(places + partners)
    copies = []

    def block(order_to, ens_to):
        return gradient.at[pl.ds(ens_to * members, members), pl.ds(order_to * rows, rows)]

    def share(core_to, ens_to):
        return weight_grad.at[:, pl.ds((core_to * enses + ens_to) * part, part)]

    home_to = home.at[
        :, :, pl.ds(pl.multiple_of((order * enses + ens) * width, LANES), width)
    ]
    share_to = shares.at[core * enses + ens]
    fellows = partners + [(core, order, lax.rem(ens + step, enses)) for step in range(1, enses)]
    for step, place in enumerate(fellows):
        copies.append(
            pltpu.make_async_remote_copy(
                share(place[0], place[2]), share_to, send_share.at[step], recv_share.at[step],
                device_id=place, device_id_type=MESH,
            )
        )
        copies[-1].start()
    for step, place in enumerate(places):
        copies.append(
            pltpu.make_async_remote_copy(
                block(place[1], place[2]), home_to, send.at[step], recv.at[step],
                device_id=place, device_id_type=MESH,
            )
        )
        copies[-1].start()
    own = ((block(order, ens), held, home_to), (share(core, ens), held_share, share_to))
    first = [pltpu.make_async_copy(a, b, own_sem.at[0, k]) for k, (a, b, _) in enumerate(own)]
    second = [pltpu.make_async_copy(b, c, own_sem.at[1, k]) for k, (_, b, c) in enumerate(own)]
    for copy in first:
        copy.start()
    for one, two in zip(first, second):
        one.wait()
        two.start()
    for copy in second:
        copy.wait()
    for copy in copies:
        copy.wait()


def scatter_rows(orders, enses, cores, gradient, weight_grad):
    members, rows, width = gradient.shape
    members, rows = members // enses, rows // orders
    own_orders, rows_all, degrees = weight_grad.shape
    part = rows_all // (cores * enses)
    peers = orders * enses - 1
    fellows = cores * enses - 1
    anywhere = pl.BlockSpec(memory_space=pl.ANY)
    return pl.pallas_call(
        functools.partial(scatter_kernel, orders, enses),
        out_shape=(
            jax.ShapeDtypeStruct((members, rows, width * orders * enses), gradient.dtype),
            jax.ShapeDtypeStruct((cores * enses, own_orders, part, degrees), weight_grad.dtype),
        ),
        in_specs=[anywhere] * 2,
        out_specs=(anywhere,) * 2,
        scratch_shapes=[
            pltpu.VMEM((members, rows, width), gradient.dtype),
            pltpu.VMEM((own_orders, part, degrees), weight_grad.dtype),
            pltpu.SemaphoreType.DMA((peers,)),
            pltpu.SemaphoreType.DMA((peers,)),
            pltpu.SemaphoreType.DMA((fellows,)),
            pltpu.SemaphoreType.DMA((fellows,)),
            pltpu.SemaphoreType.DMA((2, 2)),
        ],
        compiler_params=pltpu.CompilerParams(
            collective_id=1, has_side_effects=True, vmem_limit_bytes=VMEM_LIMIT
        ),
        name="scatter_rows",
    )(gradient, weight_grad)


def contract(a, b, dims, precision=None):
    return lax.dot_general(
        a, b, (dims, ((), ())), precision=precision, preferred_element_type=jnp.float32
    )


NN = ((1,), (0,))
NT = ((1,), (1,))
TN = ((0,), (0,))


def marks(shape, rule):
    row = lax.broadcasted_iota(jnp.int32, shape, 0)
    column = lax.broadcasted_iota(jnp.int32, shape, 1)
    return rule(row, column)


def as_float(flags):
    return jnp.where(flags, 1.0, 0.0).astype(jnp.float32)


def same_degree():
    return marks((ROWS, ROWS), lambda r, c: lax.rem(r, BLOCK) == lax.rem(c, BLOCK))


def same_member():
    return marks((ROWS, ROWS), lambda r, c: r // BLOCK == c // BLOCK)


def spread_bands(hot, rows_are_degrees):
    repeat_band = as_float(marks((ROWS, LANES), lambda r, c: lax.rem(r, BLOCK) == c))
    repeat_degree = as_float(marks((ROWS, BLOCK), lambda r, c: lax.rem(r, BLOCK) == c))
    if rows_are_degrees:
        wide = contract(repeat_degree, hot, NN)
        full = contract(wide, repeat_band, NT)
    else:
        wide = contract(repeat_band, hot, NT)
        full = contract(wide, repeat_degree, NT)
    return jnp.where(same_member(), full, 0.0)


def stack_members(ref, start):
    block = ref[:, pl.ds(start, BLOCK), :]
    return block.reshape(ROWS, block.shape[2])


def spectra_kernel(orders, enses, own_orders, grid, weights, observed, bands, spec, sums, pairs, cross):
    step = pl.program_id(0)
    order_start = (lax.axis_index("order") * enses + lax.axis_index("ens")) * own_orders
    degrees = spec.shape[1]
    blocks = degrees // BLOCK

    @pl.when(step == 0)
    def _():
        pairs[...] = jnp.zeros_like(pairs)
        cross[...] = jnp.zeros_like(cross)

    for k in range(PAIR):
        keep = (
            lax.broadcasted_iota(jnp.int32, (degrees, 2 * LANES), 0)
            >= order_start + step * PAIR + k
        )
        matrix = weights[k]
        lanes = slice(k * LANES, (k + 1) * LANES)
        for i in range(0, MEMBERS, 2):
            values = jnp.concatenate([grid[i, :, lanes], grid[i + 1, :, lanes]], axis=1)
            out = contract(matrix, values, TN)
            out = jnp.where(keep, out, 0.0).astype(jnp.bfloat16)
            spec[i, :, lanes] = out[:, :LANES]
            spec[i + 1, :, lanes] = out[:, LANES:]

    @pl.loop(0, blocks)
    def _(block):
        start = pl.multiple_of(block * BLOCK, BLOCK)
        member_rows = stack_members(spec, start)
        row = lax.broadcasted_iota(jnp.int32, (BLOCK, PAIR * LANES), 0) + start
        column = lax.broadcasted_iota(jnp.int32, (BLOCK, PAIR * LANES), 1) // LANES
        seen = observed[pl.ds(start, BLOCK), :]
        seen = jnp.where(row >= order_start + step * PAIR + column, seen.astype(jnp.float32), 0.0)
        seen = seen.astype(jnp.bfloat16)
        pairs[block] += contract(member_rows, member_rows, NT)
        cross[block, :, :ROWS] += contract(seen, member_rows, NT)
        cross[block, :, ROWS:] += contract(seen, jnp.concatenate([seen] * 8, axis=0), NT)

    @pl.when(step == pl.num_programs(0) - 1)
    def _():
        sums[...] = jnp.zeros_like(sums)
        pick_member = as_float(marks((MEMBERS, ROWS), lambda r, c: r == c // BLOCK))
        pick_degree = marks((BLOCK, ROWS), lambda r, c: r == lax.rem(c, BLOCK))
        pick_own = marks((BLOCK, LANES), lambda r, c: r == c)

        @pl.loop(0, blocks)
        def _(block):
            start = pl.multiple_of(block * BLOCK, BLOCK)
            hot = bands[pl.ds(start, BLOCK), :]
            banded = spread_bands(hot, False)
            matched = jnp.where(same_degree(), pairs[block], 0.0)
            per_degree = contract(pick_member, matched, NN, HIGHEST)
            with_obs = jnp.sum(
                jnp.where(pick_degree, cross[block, :, :ROWS], 0.0), axis=0, keepdims=True
            )
            own_obs = jnp.sum(
                jnp.where(pick_own, cross[block, :, ROWS:], 0.0), axis=1, keepdims=True
            )
            sums[:MEMBERS, :] += contract(per_degree, banded, NT, HIGHEST)
            sums[MEMBERS : MEMBERS + 8, :] += contract(
                jnp.broadcast_to(with_obs, (8, ROWS)), banded, NT, HIGHEST
            )
            sums[MEMBERS + 8 :, :LANES] += jnp.broadcast_to(
                jnp.sum(hot * own_obs, axis=0, keepdims=True), (8, LANES)
            )


def spectra_call(orders, enses, grid, weights, observed, bands):
    members, rows, width = grid.shape
    own_orders = width // LANES
    degrees = observed.shape[0]
    blocks = degrees // BLOCK
    steps = own_orders // PAIR
    return pl.pallas_call(
        functools.partial(spectra_kernel, orders, enses, own_orders),
        grid=(steps,),
        out_shape=(
            jax.ShapeDtypeStruct((members, degrees, width), grid.dtype),
            jax.ShapeDtypeStruct((MEMBERS + 16, ROWS), jnp.float32),
        ),
        in_specs=[
            pl.BlockSpec((members, rows, PAIR * LANES), lambda s: (0, 0, s)),
            pl.BlockSpec((PAIR, rows, degrees), lambda s: (s, 0, 0)),
            pl.BlockSpec((degrees, PAIR * LANES), lambda s: (0, s)),
            pl.BlockSpec((degrees, LANES), lambda s: (0, 0)),
        ],
        out_specs=(
            pl.BlockSpec((members, degrees, PAIR * LANES), lambda s: (0, 0, s)),
            pl.BlockSpec((MEMBERS + 16, ROWS), lambda s: (0, 0)),
        ),
        scratch_shapes=[
            pltpu.VMEM((blocks, ROWS, ROWS), jnp.float32),
            pltpu.VMEM((blocks, BLOCK, ROWS + LANES), jnp.float32),
        ],
        compiler_params=pltpu.CompilerParams(vmem_limit_bytes=VMEM_LIMIT),
        name="spectra",
    )(grid, weights, observed, bands)


def gradient_kernel(
    enses, own_orders, grid, spec, weights, observed, bands, mixing, out, weight_grad,
    high, low, coefficients, mixed
):
    step = pl.program_id(0)
    order_start = (lax.axis_index("order") * enses + lax.axis_index("ens")) * own_orders
    degrees = spec.shape[1]
    blocks = degrees // BLOCK

    @pl.when(step == 0)
    def _():
        place_member = as_float(marks((LANES, ROWS), lambda r, c: r == c // BLOCK))

        @pl.loop(0, blocks)
        def _(block):
            start = pl.multiple_of(block * BLOCK, BLOCK)
            hot = bands[pl.ds(start, BLOCK), :]
            banded = spread_bands(hot, True)
            own = contract(banded, mixing[...], NN, HIGHEST)
            full = jnp.where(same_degree(), contract(own, place_member, NN, HIGHEST), 0.0)
            top = full.astype(jnp.bfloat16)
            high[block] = top
            low[block] = (full - top.astype(jnp.float32)).astype(jnp.bfloat16)
            coefficients[block] = jnp.broadcast_to(
                own[:, MEMBERS : MEMBERS + 1], (ROWS, LANES)
            )

    @pl.loop(0, blocks)
    def _(block):
        start = pl.multiple_of(block * BLOCK, BLOCK)
        member_rows = stack_members(spec, start)
        row = lax.broadcasted_iota(jnp.int32, (BLOCK, PAIR * LANES), 0) + start
        column = lax.broadcasted_iota(jnp.int32, (BLOCK, PAIR * LANES), 1) // LANES
        seen = observed[pl.ds(start, BLOCK), :].astype(jnp.float32)
        seen = jnp.where(row >= order_start + step * PAIR + column, seen, 0.0)
        total = contract(high[block], member_rows, NN) + contract(low[block], member_rows, NN)
        factor = coefficients[block].reshape(MEMBERS, BLOCK, LANES)
        factor = jnp.concatenate([factor] * PAIR, axis=2)
        total = total.reshape(MEMBERS, BLOCK, PAIR * LANES) + factor * seen[None]
        mixed[:, pl.ds(start, BLOCK), :] = total.astype(jnp.bfloat16)

    for k in range(PAIR):
        matrix = weights[k]
        lanes = slice(k * LANES, (k + 1) * LANES)
        slope = jnp.zeros((matrix.shape[0], degrees), jnp.float32)
        for i in range(0, MEMBERS, 2):
            both = jnp.concatenate([mixed[i, :, lanes], mixed[i + 1, :, lanes]], axis=1)
            values = jnp.concatenate([grid[i, :, lanes], grid[i + 1, :, lanes]], axis=1)
            rows = contract(matrix, both, NN).astype(jnp.bfloat16)
            out[i, :, lanes] = rows[:, :LANES]
            out[i + 1, :, lanes] = rows[:, LANES:]
            slope += contract(values, both, NT)
        weight_grad[k] = (slope * WEIGHT_RATIO).astype(jnp.bfloat16)


def gradient_call(enses, grid, spec, weights, observed, bands, mixing):
    members, rows, width = grid.shape
    own_orders = width // LANES
    degrees = observed.shape[0]
    blocks = degrees // BLOCK
    steps = own_orders // PAIR
    return pl.pallas_call(
        functools.partial(gradient_kernel, enses, own_orders),
        grid=(steps,),
        out_shape=(
            jax.ShapeDtypeStruct((members, rows, width), grid.dtype),
            jax.ShapeDtypeStruct((own_orders, rows, degrees), grid.dtype),
        ),
        in_specs=[
            pl.BlockSpec((members, rows, PAIR * LANES), lambda s: (0, 0, s)),
            pl.BlockSpec((members, degrees, PAIR * LANES), lambda s: (0, 0, s)),
            pl.BlockSpec((PAIR, rows, degrees), lambda s: (s, 0, 0)),
            pl.BlockSpec((degrees, PAIR * LANES), lambda s: (0, s)),
            pl.BlockSpec((degrees, LANES), lambda s: (0, 0)),
            pl.BlockSpec((ROWS, LANES), lambda s: (0, 0)),
        ],
        out_specs=(
            pl.BlockSpec((members, rows, PAIR * LANES), lambda s: (0, 0, s)),
            pl.BlockSpec((PAIR, rows, degrees), lambda s: (s, 0, 0)),
        ),
        scratch_shapes=[
            pltpu.VMEM((blocks, ROWS, ROWS), jnp.bfloat16),
            pltpu.VMEM((blocks, ROWS, ROWS), jnp.bfloat16),
            pltpu.VMEM((blocks, ROWS, LANES), jnp.float32),
            pltpu.VMEM((members, degrees, PAIR * LANES), jnp.bfloat16),
        ],
        compiler_params=pltpu.CompilerParams(vmem_limit_bytes=VMEM_LIMIT),
        name="gradient",
    )(grid, spec, weights, observed, bands, mixing)


def grams_of(sums):
    among = sums[:MEMBERS].reshape(MEMBERS, MEMBERS, NBANDS)
    with_obs = sums[MEMBERS].reshape(1, MEMBERS, NBANDS)
    own_obs = sums[MEMBERS + 8, :NBANDS].reshape(1, 1, NBANDS)
    top = jnp.concatenate([among, with_obs], axis=0)
    column = jnp.concatenate([with_obs, own_obs], axis=1)
    column = jnp.transpose(column, (1, 0, 2))
    full = jnp.concatenate([top, column], axis=1)
    return jnp.transpose(full, (2, 0, 1))[None]


def kernel_body(fourier, analysis, target, band_ids, partners, band_cotangent):
    samples = fourier.shape[0]
    orders = lax.axis_size("order")
    enses = lax.axis_size("ens")
    cores = lax.axis_size("dp")
    own_orders = analysis.shape[1] // enses
    core, order, ens = my_place()

    weights = lax.dynamic_slice_in_dim(analysis, ens * own_orders, own_orders, 1)
    weights = jnp.transpose(weights, (1, 0, 2))
    band_range = jnp.arange(LANES, dtype=jnp.int32)
    onehot = (band_ids[:, :1] == band_range[None, :]).astype(jnp.float32)
    grid, observed, bands = gather_rows(orders, enses, fourier[0], target[0], onehot)
    spec, sums = spectra_call(orders, enses, grid, weights, observed, bands)
    sums = lax.psum(sums, ("order", "ens"))
    grams = grams_of(sums)
    cotangent = lax.dynamic_slice_in_dim(band_cotangent, core * samples, samples, 0)
    scores, mixing = band_terms(grams, partners, cotangent)
    loss_bands = lax.psum(jnp.sum(cotangent * scores, axis=0), "dp")
    table = jnp.transpose(mixing[0], (1, 0, 2)).reshape(ROWS, MEMBERS + 1)
    table = jnp.pad(table, ((0, 0), (0, LANES - MEMBERS - 1)))
    gradient, weight_grad = gradient_call(enses, grid, spec, weights, observed, bands, table)
    home, shares = scatter_rows(orders, enses, cores, gradient, weight_grad)
    shares = shares.reshape((cores, enses) + shares.shape[1:]).astype(jnp.float32)
    total = jnp.transpose(jnp.sum(shares, axis=0), (2, 0, 1, 3))
    grad_analysis = total.reshape(total.shape[0], -1, total.shape[3])
    return (home[None], grad_analysis, loss_bands)


def solution(mesh):
    placed = (
        P("dp", "ens", "order", None),
        P(None, "order", None),
        P("dp", "ens", "order"),
        P("ens", "order"),
        P(),
        P(),
    )
    groups = mesh.shape["order"] * mesh.shape["ens"]
    rows = NLAT // mesh.shape["order"]
    own_orders = L // groups
    fits = (
        L % (groups * PAIR) == 0
        and rows % 8 == 0
        and L % (BLOCK * mesh.shape["ens"]) == 0
        and NLAT % (mesh.shape["dp"] * mesh.shape["ens"] * 8) == 0
        and mesh.shape["dp"] == 2
    )
    return jax.shard_map(
        kernel_body if fits else body,
        mesh=mesh,
        in_specs=placed,
        out_specs=(P("dp", "ens", "order", None), P(("dp", "ens"), "order", None), P()),
        check_vma=False,
    )
```
